32 devices in a mesh: row: 2 (over x), col: 4 (over z), box: 4 (over y, core).
Axes of the slice: x: 2, y: 2, z: 4, core: 2. Of those that a mesh axis runs over, the one named last changes fastest.
Arguments:
- coeffs: bfloat16 [81920, 512], P(('row', 'box'), 'col'), may hold values from -6 to 6
- reflectors: bfloat16 [81920, 256], P(('row', 'box')), may hold values from -0.078125 to 0.078125
- factor: float32 [256, 256], replicated, may hold values from -0.375 to 0.375
- func_exp: float32 [81920], replicated, may hold values from 0.5 to 20
- func_atom: int32 [81920], replicated, may hold values from 0 to 8191, never falling along the last dimension, each value on 1 to 20 neighbouring positions
- atom_pos: float32 [3, 8192], replicated, may hold values from 0 to 1
- point_pos: float32 [3, 128, 128], P(None, ('row', 'col', 'box')), may hold values from 0 to 1
- send_tiles: int32 [8, 8, 2], replicated, may hold values from 0 to 79, as said below
- box_tiles: int32 [128, 16], P(('row', 'col', 'box')), may hold values from 0 to 15, as said below
- box_count: int32 [128], P(('row', 'col', 'box')), may hold values from 1 to 16
Outputs:
- rotated: bfloat16 [81920, 512], P(('row', 'box'), 'col')
- density: float32 [128, 128], P(('row', 'col', 'box'))
The draws below stay inside these ranges and needn't reach their ends.
Inputs may be any that keep to these rules, and one draw needn't show every extreme that they name: `send_tiles`: for each basis group and box group the 2 tiles are different local tiles of the basis group. `box_tiles`: the 16 slots listed by a box are different. `func_atom`: never falls along the basis functions; every atom carries 1 to 20 functions.
All inputs are finite; a program needn't handle non-finite values.
Results may differ from the reference program's by a relative error of at most 0.015.
Values may be sent and summed in bfloat16 or wider, within the bound.
A program may use at most 128 MiB of HBM per device.

```python
import math
import jax
import jax.numpy as jnp
import numpy as np
from jax import lax

NB = 81920
K = 512
NREF = 256
NATOM = 8192
TILE = 128
PTS = 128
TPB = 16
CAP = 2
BOX_DEV = 4
NPEER = 8
TL = 80
NBOXES = 128
N_COL = 4
N_BOX = 4


def draw_send_tiles(key, part):
    keys = jax.random.split(key, NPEER * NPEER)
    picks = jax.vmap(lambda one: jax.random.permutation(one, TL)[:CAP])(keys)
    picks = picks.reshape(NPEER, NPEER, CAP).astype(jnp.int32)
    picks = picks.at[0, 0, :].set(jnp.arange(CAP, dtype=jnp.int32) + TL - CAP)
    picks = picks.at[0, 1, :].set(jnp.arange(CAP, dtype=jnp.int32))
    return picks


def draw_box_tiles(key, part):
    slots = NPEER * CAP
    keys = jax.random.split(key, NBOXES)
    picks = jax.vmap(lambda one: jax.random.permutation(one, slots)[:TPB])(keys).astype(jnp.int32)
    picks = picks.at[0, :].set(jnp.arange(TPB, dtype=jnp.int32))
    picks = picks.at[1, :].set(slots - 1 - jnp.arange(TPB, dtype=jnp.int32))
    return picks


def place_ends(drawn, stream_key, smallest, top_value):
    longest = drawn.shape.index(max(drawn.shape))
    spots = []
    for shift in (0, 1):
        where = [jax.random.randint(jax.random.fold_in(stream_key, axis), (), 0, length) for axis, length in enumerate(drawn.shape)]
        where[longest] = (where[longest] + shift) % drawn.shape[longest]
        spots.append(tuple(where))
    return drawn.at[spots[0]].set(smallest).at[spots[1]].set(top_value)


def shard_levels(key, shape, shards, least, high):
    def one(axis_at, parts):
        steps = jax.random.uniform(jax.random.fold_in(jax.random.fold_in(key, 6), axis_at), (parts,), jnp.float32, least / len(shards), high / len(shards))
        return jnp.repeat(jnp.exp(steps), shape[axis_at] // parts).reshape((-1,) + (1,) * (len(shape) - axis_at - 1))

    level = one(*shards[0])
    for cut in shards[1:]:
        level = level * one(*cut)
    return level


def split_up(number_of, total, reach, skew):
    weights = [(1 << 20) // math.isqrt(standing ** skew) + 1 for standing in range(2, number_of + 1)]
    spare, counts = total - reach - (number_of - 1), [1] * (number_of - 1)
    while spare > 0:
        free = [i for i in range(number_of - 1) if counts[i] < reach]
        whole, budget = sum([weights[i] for i in free]), spare
        for i in free:
            extra = min(reach - counts[i], max(1, budget * weights[i] // whole), spare)
            counts[i] = counts[i] + extra
            spare = spare - extra
    return np.array([reach] + counts)


def ragged(own_key, number_of, total, reach, skew):
    if number_of == 2:
        one = jax.random.randint(own_key, (), max(1, total - reach), min(reach, total - 1) + 1)
        return jnp.stack([one, total - one])
    sizes = jnp.asarray(split_up(number_of, total, reach, skew), jnp.int32)
    couples = (number_of - 1) // 2
    donor, receiver = sizes[1:1 + 2 * couples:2], sizes[2:2 + 2 * couples:2]
    slack = jnp.minimum(donor - 1, reach - receiver)
    moved = jax.random.randint(jax.random.fold_in(own_key, 1), (couples,), 0, 1 << 20) % (slack + 1)
    sizes = sizes.at[1:1 + 2 * couples:2].set(donor - moved).at[2:2 + 2 * couples:2].set(receiver + moved)
    return sizes[jax.random.permutation(jax.random.fold_in(own_key, 2), number_of)]


def gaussian(rng, dims, scale, limit, cuts=(), held_as=jnp.bfloat16):
    values = scale * jax.random.normal(rng, dims, jnp.float32)
    if cuts:
        values = values * shard_levels(rng, dims, cuts, -0.22, 0.18)
    return jnp.clip(values, -limit, limit).astype(held_as)


def setup_inputs(seed: int = 0) -> dict:
    key_of = jax.random.split(jax.random.key(seed), 11)
    coeffs = gaussian(key_of[0], (NB, K), 1.0, 6.0, ((0, 8), (1, 4)))
    reflectors = gaussian(key_of[1], (NB, NREF), (NB // 16) ** -0.5, 0.078125, ((0, 8),))
    factor = gaussian(key_of[2], (NREF, NREF), NREF ** -0.5, 0.375, (), jnp.float32)
    func_exp = jnp.clip(jnp.exp(jax.random.uniform(key_of[3], (NB,), jnp.float32, math.log(0.5), math.log(20.0))), 0.5, 20.0)
    func_atom = jnp.searchsorted(jnp.cumsum(ragged(key_of[4], NATOM, NB, 20, 0)), jnp.arange(NB), side="right").astype(jnp.int32)
    atom_pos = jnp.clip(jax.random.uniform(key_of[5], (3, NATOM), jnp.float32, 0.0, 1.0), 0.0, 1.0)
    point_pos = jnp.clip(1.0 * jax.random.uniform(key_of[6], (3, NBOXES, PTS), jnp.float32) ** shard_levels(key_of[6], (3, NBOXES, PTS), ((1, 32),), -0.2, 0.2), 0.0, 1.0)
    send_tiles = draw_send_tiles(jax.random.fold_in(key_of[10], 71), 0)
    box_tiles = draw_box_tiles(jax.random.fold_in(key_of[10], 71), 0)
    box_count = place_ends(jax.random.randint(key_of[9], (NBOXES,), 1, TPB + 1), jax.random.fold_in(key_of[9], 1), 1, TPB).astype(jnp.int32)
    return {"coeffs": coeffs, "reflectors": reflectors, "factor": factor, "func_exp": func_exp, "func_atom": func_atom, "atom_pos": atom_pos, "point_pos": point_pos, "send_tiles": send_tiles, "box_tiles": box_tiles, "box_count": box_count}


def reference(coeffs, reflectors, factor, func_exp, func_atom, atom_pos, point_pos, send_tiles, box_tiles, box_count):
    panel = jnp.dot(reflectors.T, coeffs, preferred_element_type=jnp.float32)
    scaled = jnp.dot(factor, panel, precision=lax.Precision.HIGHEST).astype(jnp.bfloat16)
    rotated = (coeffs.astype(jnp.float32) - jnp.dot(reflectors, scaled, preferred_element_type=jnp.float32)).astype(jnp.bfloat16)
    offsets = jnp.arange(TILE, dtype=jnp.int32)
    positions = jnp.arange(TPB, dtype=jnp.int32)

    def one_box(items):
        number, listed, count, points = items
        device = number // BOX_DEV
        group = (device // (N_COL * N_BOX)) * N_BOX + device % N_BOX
        source = listed // CAP
        within = listed % CAP
        tile = source * TL + send_tiles[source, group, within]
        funcs = tile[:, None] * TILE + offsets[None, :]
        alpha = func_exp[funcs]
        centre = atom_pos[:, func_atom[funcs]]
        first = points[0][:, None, None] - centre[0][None]
        dist = first * first
        second = points[1][:, None, None] - centre[1][None]
        dist = dist + second * second
        third = points[2][:, None, None] - centre[2][None]
        dist = dist + third * third
        live = positions < count
        phi = jnp.where(live[None, :, None], jnp.exp(-alpha[None] * dist), 0.0).astype(jnp.bfloat16)
        phi = phi.reshape(PTS, TPB * TILE)
        block = rotated[funcs.reshape(-1)]
        orbital = jnp.dot(phi, block, preferred_element_type=jnp.float32)
        return jnp.sum(orbital * orbital, 1) / (K * TILE)

    numbers = jnp.arange(NBOXES, dtype=jnp.int32)
    density = lax.map(one_box, (numbers, box_tiles, box_count, jnp.moveaxis(point_pos, 1, 0)))
    return rotated, density
```

```python
import functools
import math

import jax
import jax.numpy as jnp
from jax import lax
from jax.experimental import pallas as pl
from jax.experimental.pallas import tpu as pltpu
from jax.sharding import PartitionSpec as P

K = 512
TILE = 128


def box_density(arrived, slot_alpha, slot_centre, listed, count, points):
    alpha = slot_alpha[listed]
    centre = slot_centre[:, listed]
    first = points[0][:, None, None] - centre[0][None]
    dist = first * first
    second = points[1][:, None, None] - centre[1][None]
    dist = dist + second * second
    third = points[2][:, None, None] - centre[2][None]
    dist = dist + third * third
    live = jnp.arange(listed.shape[0], dtype=jnp.int32) < count
    phi = jnp.where(live[None, :, None], jnp.exp(-alpha[None] * dist), 0.0).astype(jnp.bfloat16)
    phi = phi.reshape(points.shape[1], -1)
    block = arrived[listed].reshape(-1, arrived.shape[2])
    orbital = jnp.dot(phi, block, preferred_element_type=jnp.float32)
    return jnp.sum(orbital * orbital, 1) / (K * TILE)


def by_blocks(arrived, slot_alpha, slot_centre, lists, counts, points):
    boxes = lists.shape[0]
    width = math.gcd(boxes, 2)
    steps = boxes // width
    lists_blocked = lists.reshape(steps, width, lists.shape[1])
    counts_blocked = counts.reshape(steps, width)
    moved = jnp.moveaxis(points, 1, 0)
    points_blocked = moved.reshape(steps, width, moved.shape[1], moved.shape[2])
    single = jax.vmap(
        lambda listed, count, where: box_density(
            arrived, slot_alpha, slot_centre, listed, count, where
        )
    )

    def one_block(items):
        return single(items[0], items[1], items[2])

    result = lax.map(one_block, (lists_blocked, counts_blocked, points_blocked))
    return result.reshape(boxes, result.shape[2])


def general(
    coeffs,
    reflectors,
    factor,
    func_exp,
    func_atom,
    atom_pos,
    point_pos,
    send_tiles,
    box_tiles,
    box_count,
):
    panel_part = jnp.dot(reflectors.T, coeffs, preferred_element_type=jnp.float32)
    panel = lax.psum(panel_part.astype(jnp.bfloat16), ("row", "box")).astype(jnp.float32)
    scaled = jnp.dot(factor, panel, precision=lax.Precision.HIGHEST).astype(jnp.bfloat16)
    rotated = (
        coeffs.astype(jnp.float32) - jnp.dot(reflectors, scaled, preferred_element_type=jnp.float32)
    ).astype(jnp.bfloat16)
    peers = lax.axis_size(("row", "box"))
    group = lax.axis_index(("row", "box"))
    capacity = send_tiles.shape[2]
    local_tiles = coeffs.shape[0] // TILE
    slots = jnp.arange(peers * capacity, dtype=jnp.int32)
    source = slots // capacity
    within = slots % capacity
    tile = source * local_tiles + send_tiles[source, group, within]
    funcs = tile[:, None] * TILE + jnp.arange(TILE, dtype=jnp.int32)[None, :]
    slot_alpha = func_exp[funcs]
    slot_centre = atom_pos[:, func_atom[funcs]]
    outgoing_index = send_tiles[group]
    outgoing = rotated.reshape(local_tiles, TILE, rotated.shape[1])[outgoing_index]
    arrived = lax.all_to_all(outgoing, ("row", "box"), split_axis=0, concat_axis=0, tiled=True)
    arrived = arrived.reshape(peers * capacity, TILE, arrived.shape[3])
    lists, counts = (
        lax.all_gather(box_tiles, "col", axis=0, tiled=True),
        lax.all_gather(box_count, "col", axis=0, tiled=True),
    )
    points = lax.all_gather(point_pos, "col", axis=1, tiled=True)
    partial_value = by_blocks(arrived, slot_alpha, slot_centre, lists, counts, points)
    density = lax.psum_scatter(
        partial_value.astype(jnp.bfloat16), "col", scatter_dimension=0, tiled=True
    ).astype(jnp.float32)
    return (rotated, density)


MESH = pl.DeviceIdType.MESH
LANES = 128
LOAD = 1024
EMIT = 1024


def prepare(
    n_box, coeffs_hbm, refl_hbm, alpha_ref, atom_ref, pos_ref, point_ref, send_ref, list_ref,
    count_ref, slot_info, info_ref, picked_c, picked_r, window, pick_sem
):
    f32 = jnp.float32
    me = lax.axis_index("row") * n_box + lax.axis_index("box")
    slots, capacity = slot_info.shape[0], send_ref.shape[2]
    boxes = list_ref.shape[0]
    tiles = coeffs_hbm.shape[0] // TILE

    def picks(s):
        tile = send_ref[me, s // capacity, s % capacity]
        source = pl.ds(pl.multiple_of(tile * TILE, TILE), TILE)
        target = pl.ds(s * TILE, TILE)
        return (
            pltpu.make_async_copy(coeffs_hbm.at[source], picked_c.at[target], pick_sem.at[2 * s]),
            pltpu.make_async_copy(refl_hbm.at[source], picked_r.at[target], pick_sem.at[2 * s + 1]),
        )

    for s in range(slots):
        for copy in picks(s):
            copy.start()

    lane = lax.broadcasted_iota(jnp.int32, (1, LANES), 1)
    info = [point_ref[c] for c in range(3)]
    for b in range(boxes):
        live = jnp.zeros((1, LANES), f32)
        for i in range(list_ref.shape[1]):
            used = jnp.where(i < count_ref[b], list_ref[b, i], -1)
            live = jnp.where(lane == used, 1.0, live)
        info.append(live)
    info_ref[...] = jnp.concatenate(info, axis=0)

    window[...] = jnp.zeros_like(window)
    last = pos_ref.shape[1] // LANES - 1
    depth = lax.broadcasted_iota(jnp.int32, (2 * LANES, LANES), 0)

    for s in range(slots):
        q, j = s // capacity, s % capacity
        tile = q * tiles + send_ref[q, me, j]
        atoms = atom_ref[pl.ds(tile, 1), :]
        block = jnp.min(atoms) // LANES
        after = jnp.minimum(block + 1, last)
        window[s, 0:3, 0:LANES] = pos_ref[:, pl.ds(pl.multiple_of(block * LANES, LANES), LANES)]
        window[s, 0:3, LANES:] = pos_ref[:, pl.ds(pl.multiple_of(after * LANES, LANES), LANES)]
        pick = jnp.where(depth == atoms - block * LANES, 1.0, 0.0)
        slot_info[s, 0:8, :] = jnp.dot(
            window[s], pick, precision=lax.Precision.HIGHEST, preferred_element_type=f32
        )
        slot_info[s, 3:4, :] = -alpha_ref[pl.ds(tile, 1), :]

    for s in range(slots):
        for copy in picks(s):
            copy.wait()


def kernel(
    n_row,
    n_box,
    n_col,
    coeffs_hbm,
    refl_hbm,
    factor_ref,
    slot_info,
    info_ref,
    picked_c,
    picked_r,
    rot_hbm,
    dens_ref,
    coeffs_v,
    refl_v,
    rot_v,
    part_f,
    part_b,
    got1,
    scaled_t,
    outbox,
    arrived,
    box_info,
    planes,
    phi,
    dens_own,
    dens_got,
    load_sem,
    emit_sem,
    info_send,
    info_recv,
    sum_send,
    sum_recv,
    gather_send,
    gather_recv,
    tile_send,
    tile_recv,
    dens_send,
    dens_recv,
):
    f32, bf16 = jnp.float32, jnp.bfloat16
    peers = n_row * n_box
    row, box, col = lax.axis_index("row"), lax.axis_index("box"), lax.axis_index("col")
    me = row * n_box + box
    rows, width = coeffs_v.shape
    loads = rows // LOAD
    emits = rows // EMIT
    share = width // peers
    slots = slot_info.shape[0]
    capacity = slots // peers
    boxes = dens_ref.shape[0]

    def load(i):
        at = pl.ds(i * LOAD, LOAD)
        return (
            pltpu.make_async_copy(coeffs_hbm.at[at], coeffs_v.at[at], load_sem.at[2 * i]),
            pltpu.make_async_copy(refl_hbm.at[at], refl_v.at[at], load_sem.at[2 * i + 1]),
        )

    for i in range(loads):
        for copy in load(i):
            copy.start()

    def in_plane(d):
        peer = lax.rem(me + d, peers)
        return peer, {"row": peer // n_box, "box": lax.rem(peer, n_box)}

    def in_col(d):
        peer = lax.rem(col + d, n_col)
        return peer, {"col": peer}

    barrier = pltpu.get_barrier_semaphore()
    for d in range(1, peers):
        pl.semaphore_signal(barrier, inc=1, device_id=in_plane(d)[1], device_id_type=MESH)
    for d in range(1, n_col):
        pl.semaphore_signal(barrier, inc=1, device_id=in_col(d)[1], device_id_type=MESH)

    mine = pl.ds(pl.multiple_of(col * 16, 16), 16)
    box_info[mine, :] = info_ref[...]

    pl.semaphore_wait(barrier, peers - 1 + n_col - 1)

    info_copies = []
    for d in range(1, n_col):
        copy = pltpu.make_async_remote_copy(
            src_ref=box_info.at[mine],
            dst_ref=box_info.at[mine],
            send_sem=info_send.at[d],
            recv_sem=info_recv.at[d],
            device_id=in_col(d)[1],
            device_id_type=MESH,
        )
        copy.start()
        info_copies.append(copy)

    part_f[...] = jnp.zeros_like(part_f)

    @pl.loop(0, loads)
    def _(i):
        for copy in load(i):
            copy.wait()
        at = pl.ds(pl.multiple_of(i * LOAD, LOAD), LOAD)
        part_f[...] += lax.dot_general(
            coeffs_v[at, :], refl_v[at, :], (((0,), (0,)), ((), ())), preferred_element_type=f32
        )

    part_b[...] = part_f[...].astype(bf16)
    sum_copies = []
    for d in range(1, peers):
        peer, where = in_plane(d)
        copy = pltpu.make_async_remote_copy(
            src_ref=part_b.at[pl.ds(pl.multiple_of(peer * share, share), share)],
            dst_ref=got1.at[d],
            send_sem=sum_send.at[d],
            recv_sem=sum_recv.at[d],
            device_id=where,
            device_id_type=MESH,
        )
        copy.start()
        sum_copies.append(copy)

    for copy in info_copies:
        copy.wait()
    turned = jnp.concatenate(
        [box_info[...], jnp.zeros((LANES - box_info.shape[0], LANES), f32)], axis=0
    ).T
    for j in range(n_col):
        for b in range(boxes):
            for c in range(4):
                k = j * 16 + c * boxes + b
                planes[j * boxes + b, c] = jnp.broadcast_to(turned[:, k : k + 1], (LANES, LANES))

    def fill(first, count):
        @pl.loop(first, first + count)
        def _(n):
            at = pl.ds(pl.multiple_of(n * LANES, LANES), LANES)

            @pl.loop(0, slots)
            def _(s):
                one = planes[n, 0] - slot_info[s, 0:1, :]
                dist = one * one
                two = planes[n, 1] - slot_info[s, 1:2, :]
                dist = dist + two * two
                three = planes[n, 2] - slot_info[s, 2:3, :]
                dist = dist + three * three
                value = jnp.exp(slot_info[s, 3:4, :] * dist)
                value = jnp.where(planes[n, 3, pl.ds(s, 1), :] > 0.0, value, 0.0)
                phi[at, pl.ds(pl.multiple_of(s * LANES, LANES), LANES)] = value.astype(bf16)

    fill(0, FILLS[0])

    own = pl.ds(pl.multiple_of(me * share, share), share)
    total = part_f[own, :]
    for d in range(1, peers):
        sum_copies[d - 1].wait()
        total = total + got1[d].astype(f32)
    scaled_t[own, :] = lax.dot_general(
        total,
        factor_ref[...],
        (((1,), (1,)), ((), ())),
        precision=lax.Precision.HIGHEST,
        preferred_element_type=f32,
    ).astype(bf16)
    gather_copies = []
    for d in range(1, peers):
        copy = pltpu.make_async_remote_copy(
            src_ref=scaled_t.at[own],
            dst_ref=scaled_t.at[own],
            send_sem=gather_send.at[d],
            recv_sem=gather_recv.at[d],
            device_id=in_plane(d)[1],
            device_id_type=MESH,
        )
        copy.start()
        gather_copies.append(copy)

    fill(FILLS[0], FILLS[1])

    for copy in gather_copies:
        copy.wait()

    def rotate(before, vectors):
        change = lax.dot_general(
            vectors, scaled_t[...], (((1,), (1,)), ((), ())), preferred_element_type=f32
        )
        return (before.astype(f32) - change).astype(bf16)

    span = capacity * TILE
    tile_copies = []
    here = pl.ds(pl.multiple_of(me * span, span), span)
    for d in list(range(1, peers)) + [0]:
        peer, where = in_plane(d)
        at = pl.ds(pl.multiple_of(peer * span, span), span)
        outbox[d] = rotate(picked_c[at, :], picked_r[at, :])
        if d == 0:
            arrived[here, :] = outbox[0]
            continue
        copy = pltpu.make_async_remote_copy(
            src_ref=outbox.at[d],
            dst_ref=arrived.at[here],
            send_sem=tile_send.at[d],
            recv_sem=tile_recv.at[d],
            device_id=where,
            device_id_type=MESH,
        )
        copy.start()
        tile_copies.append(copy)

    def emit(i):
        at = pl.ds(pl.multiple_of(i * EMIT, EMIT), EMIT)
        return pltpu.make_async_copy(rot_v.at[at], rot_hbm.at[at], emit_sem.at[i])

    @pl.loop(0, emits)
    def _(i):
        at = pl.ds(pl.multiple_of(i * EMIT, EMIT), EMIT)
        rot_v[at, :] = rotate(coeffs_v[at, :], refl_v[at, :])
        emit(i).start()

    done = FILLS[0] + FILLS[1]
    fill(done, n_col * boxes - done)

    for copy in tile_copies:
        copy.wait()

    lanes = lax.broadcasted_iota(jnp.int32, (LANES, LANES), 1)
    dens_copies = []
    for d in list(range(1, n_col)) + [0]:
        peer, where = in_col(d)
        tall = boxes * LANES
        at = pl.ds(pl.multiple_of(peer * tall, tall), tall)
        orbital = jnp.dot(phi[at, :], arrived[...], preferred_element_type=f32)
        summed = jnp.sum(orbital * orbital, axis=1, keepdims=True)
        spread = jnp.zeros((LANES, LANES), f32)
        for b in range(boxes):
            spread = jnp.where(lanes == b, summed[b * LANES : (b + 1) * LANES], spread)
        dens_own[d] = spread.T[0:8, :]
        if d == 0:
            continue
        copy = pltpu.make_async_remote_copy(
            src_ref=dens_own.at[d],
            dst_ref=dens_got.at[d],
            send_sem=dens_send.at[d],
            recv_sem=dens_recv.at[d],
            device_id=where,
            device_id_type=MESH,
        )
        copy.start()
        dens_copies.append(copy)
    total = dens_own[0]
    for d in range(1, n_col):
        dens_copies[d - 1].wait()
        total = total + dens_got[d]
    dens_ref[...] = total[0:boxes, :] * (1.0 / (K * TILE))

    @pl.loop(0, emits)
    def _(i):
        emit(i).wait()


FILLS = (4, 4)


def fits(coeffs, reflectors, atom_pos, point_pos, send_tiles, sizes):
    n_row, n_box, n_col = sizes
    peers = n_row * n_box
    rows, width = coeffs.shape
    boxes = point_pos.shape[1]
    slots = peers * send_tiles.shape[2]
    return (
        width == LANES
        and rows % LOAD == 0
        and rows % EMIT == 0
        and rows * (reflectors.shape[1] + 2 * width) <= 16 << 20
        and reflectors.shape[1] % LANES == 0
        and width % peers == 0
        and (width // peers) % 16 == 0
        and boxes == 4
        and n_col <= 8
        and point_pos.shape[2] == LANES
        and atom_pos.shape[1] % LANES == 0
        and slots <= LANES
        and n_col * boxes * slots <= 512
        and n_col * boxes >= FILLS[0] + FILLS[1]
    )


def per_device(
    coeffs,
    reflectors,
    factor,
    func_exp,
    func_atom,
    atom_pos,
    point_pos,
    send_tiles,
    box_tiles,
    box_count,
):
    sizes = lax.axis_size("row"), lax.axis_size("box"), lax.axis_size("col")
    if not fits(coeffs, reflectors, atom_pos, point_pos, send_tiles, sizes):
        return general(
            coeffs,
            reflectors,
            factor,
            func_exp,
            func_atom,
            atom_pos,
            point_pos,
            send_tiles,
            box_tiles,
            box_count,
        )
    n_row, n_box, n_col = sizes
    peers = n_row * n_box
    rows, width = coeffs.shape
    nref = reflectors.shape[1]
    boxes = point_pos.shape[1]
    capacity = send_tiles.shape[2]
    slots = peers * capacity
    f32, bf16 = jnp.float32, jnp.bfloat16
    vmem = pl.BlockSpec(memory_space=pltpu.VMEM)
    smem = pl.BlockSpec(memory_space=pltpu.SMEM)
    anywhere = pl.BlockSpec(memory_space=pl.ANY)
    dma = pltpu.SemaphoreType.DMA
    slot_info, info, picked_c, picked_r = pl.pallas_call(
        functools.partial(prepare, n_box),
        out_shape=(
            jax.ShapeDtypeStruct((slots, 8, LANES), f32),
            jax.ShapeDtypeStruct((4 * boxes, LANES), f32),
            jax.ShapeDtypeStruct((slots * TILE, width), bf16),
            jax.ShapeDtypeStruct((slots * TILE, nref), bf16),
        ),
        in_specs=[anywhere, anywhere, vmem, vmem, vmem, vmem, smem, smem, smem],
        out_specs=(vmem, vmem, vmem, vmem),
        scratch_shapes=[pltpu.VMEM((slots, 8, 2 * LANES), f32), dma((2 * slots,))],
        name="slot_functions",
    )(
        coeffs,
        reflectors,
        func_exp.reshape(-1, TILE),
        func_atom.reshape(-1, TILE),
        atom_pos,
        point_pos,
        send_tiles,
        box_tiles,
        box_count,
    )
    rotated, density = pl.pallas_call(
        functools.partial(kernel, n_row, n_box, n_col),
        out_shape=(
            jax.ShapeDtypeStruct((rows, width), bf16),
            jax.ShapeDtypeStruct((boxes, LANES), f32),
        ),
        in_specs=[anywhere, anywhere, vmem, vmem, vmem, vmem, vmem],
        out_specs=(anywhere, vmem),
        scratch_shapes=[
            pltpu.VMEM((rows, width), bf16),
            pltpu.VMEM((rows, nref), bf16),
            pltpu.VMEM((rows, width), bf16),
            pltpu.VMEM((width, nref), f32),
            pltpu.VMEM((width, nref), bf16),
            pltpu.VMEM((peers, width // peers, nref), bf16),
            pltpu.VMEM((width, nref), bf16),
            pltpu.VMEM((peers, capacity * TILE, width), bf16),
            pltpu.VMEM((slots * TILE, width), bf16),
            pltpu.VMEM((n_col * 16, LANES), f32),
            pltpu.VMEM((n_col * boxes, 4, LANES, LANES), f32),
            pltpu.VMEM((n_col * boxes * LANES, slots * TILE), bf16),
            pltpu.VMEM((n_col, 8, LANES), f32),
            pltpu.VMEM((n_col, 8, LANES), f32),
            dma((2 * (rows // LOAD),)),
            dma((rows // EMIT,)),
            dma((n_col,)),
            dma((n_col,)),
            dma((peers,)),
            dma((peers,)),
            dma((peers,)),
            dma((peers,)),
            dma((peers,)),
            dma((peers,)),
            dma((n_col,)),
            dma((n_col,)),
        ],
        compiler_params=pltpu.CompilerParams(
            collective_id=0, has_side_effects=True, vmem_limit_bytes=48 << 20
        ),
        name="panel_and_density",
    )(
        coeffs,
        reflectors,
        factor,
        slot_info,
        info,
        picked_c,
        picked_r,
    )
    return rotated, density


def solution(mesh):
    in_specs = (
        P(("row", "box"), "col"),
        P(("row", "box"), None),
        P(),
        P(),
        P(),
        P(),
        P(None, ("row", "col", "box"), None),
        P(),
        P(("row", "col", "box"), None),
        P(("row", "col", "box")),
    )
    out_specs = (P(("row", "box"), "col"), P(("row", "col", "box"), None))
    return jax.shard_map(
        per_device, mesh=mesh, in_specs=in_specs, out_specs=out_specs, check_vma=False
    )
```

```python
import functools
import math

import jax
import jax.numpy as jnp
from jax import lax
from jax.experimental import pallas as pl
from jax.experimental.pallas import tpu as pltpu
from jax.sharding import PartitionSpec as P

K = 512
TILE = 128


def box_density(arrived, slot_alpha, slot_centre, listed, count, points):
    alpha = slot_alpha[listed]
    centre = slot_centre[:, listed]
    first = points[0][:, None, None] - centre[0][None]
    dist = first * first
    second = points[1][:, None, None] - centre[1][None]
    dist = dist + second * second
    third = points[2][:, None, None] - centre[2][None]
    dist = dist + third * third
    live = jnp.arange(listed.shape[0], dtype=jnp.int32) < count
    phi = jnp.where(live[None, :, None], jnp.exp(-alpha[None] * dist), 0.0).astype(jnp.bfloat16)
    phi = phi.reshape(points.shape[1], -1)
    block = arrived[listed].reshape(-1, arrived.shape[2])
    orbital = jnp.dot(phi, block, preferred_element_type=jnp.float32)
    return jnp.sum(orbital * orbital, 1) / (K * TILE)


def by_blocks(arrived, slot_alpha, slot_centre, lists, counts, points):
    boxes = lists.shape[0]
    width = math.gcd(boxes, 2)
    steps = boxes // width
    lists_blocked = lists.reshape(steps, width, lists.shape[1])
    counts_blocked = counts.reshape(steps, width)
    moved = jnp.moveaxis(points, 1, 0)
    points_blocked = moved.reshape(steps, width, moved.shape[1], moved.shape[2])
    single = jax.vmap(
        lambda listed, count, where: box_density(
            arrived, slot_alpha, slot_centre, listed, count, where
        )
    )

    def one_block(items):
        return single(items[0], items[1], items[2])

    result = lax.map(one_block, (lists_blocked, counts_blocked, points_blocked))
    return result.reshape(boxes, result.shape[2])


def general(
    coeffs,
    reflectors,
    factor,
    func_exp,
    func_atom,
    atom_pos,
    point_pos,
    send_tiles,
    box_tiles,
    box_count,
):
    panel_part = jnp.dot(reflectors.T, coeffs, preferred_element_type=jnp.float32)
    panel = lax.psum(panel_part.astype(jnp.bfloat16), ("row", "box")).astype(jnp.float32)
    scaled = jnp.dot(factor, panel, precision=lax.Precision.HIGHEST).astype(jnp.bfloat16)
    rotated = (
        coeffs.astype(jnp.float32) - jnp.dot(reflectors, scaled, preferred_element_type=jnp.float32)
    ).astype(jnp.bfloat16)
    peers = lax.axis_size(("row", "box"))
    group = lax.axis_index(("row", "box"))
    capacity = send_tiles.shape[2]
    local_tiles = coeffs.shape[0] // TILE
    slots = jnp.arange(peers * capacity, dtype=jnp.int32)
    source = slots // capacity
    within = slots % capacity
    tile = source * local_tiles + send_tiles[source, group, within]
    funcs = tile[:, None] * TILE + jnp.arange(TILE, dtype=jnp.int32)[None, :]
    slot_alpha = func_exp[funcs]
    slot_centre = atom_pos[:, func_atom[funcs]]
    outgoing_index = send_tiles[group]
    outgoing = rotated.reshape(local_tiles, TILE, rotated.shape[1])[outgoing_index]
    arrived = lax.all_to_all(outgoing, ("row", "box"), split_axis=0, concat_axis=0, tiled=True)
    arrived = arrived.reshape(peers * capacity, TILE, arrived.shape[3])
    lists, counts = (
        lax.all_gather(box_tiles, "col", axis=0, tiled=True),
        lax.all_gather(box_count, "col", axis=0, tiled=True),
    )
    points = lax.all_gather(point_pos, "col", axis=1, tiled=True)
    partial_value = by_blocks(arrived, slot_alpha, slot_centre, lists, counts, points)
    density = lax.psum_scatter(
        partial_value.astype(jnp.bfloat16), "col", scatter_dimension=0, tiled=True
    ).astype(jnp.float32)
    return (rotated, density)


MESH = pl.DeviceIdType.MESH
LANES = 128
LOAD = 1024
EMIT = 1024


def kernel(
    n_row,
    n_box,
    n_col,
    coeffs_hbm,
    refl_hbm,
    factor_hbm,
    alpha_hbm,
    atom_hbm,
    pos_hbm,
    point_ref,
    send_ref,
    list_ref,
    count_ref,
    rot_hbm,
    dens_ref,
    coeffs_v,
    refl_v,
    rot_v,
    part_f,
    part_b,
    got1,
    scaled_t,
    outbox,
    arrived,
    box_info,
    planes,
    window,
    slot_info,
    phi,
    dens_own,
    dens_got,
    factor_v,
    alpha_ref,
    atom_ref,
    pos_ref,
    centres,
    table_sem,
    load_sem,
    emit_sem,
    info_send,
    info_recv,
    sum_send,
    sum_recv,
    gather_send,
    gather_recv,
    tile_send,
    tile_recv,
    dens_send,
    dens_recv,
):
    f32, bf16 = jnp.float32, jnp.bfloat16
    peers = n_row * n_box
    row, box, col = lax.axis_index("row"), lax.axis_index("box"), lax.axis_index("col")
    me = row * n_box + box
    tiles, _, width = coeffs_v.shape
    rows = tiles * TILE
    loads = rows // LOAD
    emits = rows // EMIT
    share = width // peers
    slots, capacity = slot_info.shape[0], send_ref.shape[1]
    boxes = dens_ref.shape[0]
    step = LOAD // TILE

    def load(i):
        at = pl.ds(i * step, step)
        return (
            pltpu.make_async_copy(coeffs_hbm.at[at], coeffs_v.at[at], load_sem.at[2 * i]),
            pltpu.make_async_copy(refl_hbm.at[at], refl_v.at[at], load_sem.at[2 * i + 1]),
        )

    for i in range(loads):
        for copy in load(i):
            copy.start()

    tables = [
        pltpu.make_async_copy(source, target, table_sem.at[i])
        for i, (source, target) in enumerate(
            [
                (atom_hbm, atom_ref),
                (alpha_hbm, alpha_ref),
                (pos_hbm, pos_ref),
                (factor_hbm, factor_v),
            ]
        )
    ]
    for copy in tables:
        copy.start()

    def in_plane(d):
        peer = lax.rem(me + d, peers)
        return peer, {"row": peer // n_box, "box": lax.rem(peer, n_box)}

    def in_col(d):
        peer = lax.rem(col + d, n_col)
        return peer, {"col": peer}

    barrier = pltpu.get_barrier_semaphore()
    for d in range(1, peers):
        pl.semaphore_signal(barrier, inc=1, device_id=in_plane(d)[1], device_id_type=MESH)
    for d in range(1, n_col):
        pl.semaphore_signal(barrier, inc=1, device_id=in_col(d)[1], device_id_type=MESH)

    mine = pl.ds(pl.multiple_of(col * 16, 16), 16)
    lane = lax.broadcasted_iota(jnp.int32, (1, LANES), 1)
    info = [point_ref[c] for c in range(3)]
    for b in range(boxes):
        live = jnp.zeros((1, LANES), f32)
        for i in range(list_ref.shape[1]):
            used = jnp.where(i < count_ref[b], list_ref[b, i], -1)
            live = jnp.where(lane == used, 1.0, live)
        info.append(live)
    box_info[mine, :] = jnp.concatenate(info, axis=0)

    pl.semaphore_wait(barrier, peers - 1 + n_col - 1)

    info_copies = []
    for d in range(1, n_col):
        copy = pltpu.make_async_remote_copy(
            src_ref=box_info.at[mine],
            dst_ref=box_info.at[mine],
            send_sem=info_send.at[d],
            recv_sem=info_recv.at[d],
            device_id=in_col(d)[1],
            device_id_type=MESH,
        )
        copy.start()
        info_copies.append(copy)

    part_f[...] = jnp.zeros_like(part_f)

    @pl.loop(0, loads)
    def _(i):
        for copy in load(i):
            copy.wait()
        at = pl.ds(i * step, step)
        part_f[...] += lax.dot_general(
            coeffs_v[at].reshape(LOAD, width),
            refl_v[at].reshape(LOAD, refl_v.shape[2]),
            (((0,), (0,)), ((), ())),
            preferred_element_type=f32,
        )

    part_b[...] = part_f[...].astype(bf16)
    sum_copies = []
    for d in range(1, peers):
        peer, where = in_plane(d)
        copy = pltpu.make_async_remote_copy(
            src_ref=part_b.at[pl.ds(pl.multiple_of(peer * share, share), share)],
            dst_ref=got1.at[d],
            send_sem=sum_send.at[d],
            recv_sem=sum_recv.at[d],
            device_id=where,
            device_id_type=MESH,
        )
        copy.start()
        sum_copies.append(copy)

    for copy in tables:
        copy.wait()
    window[...] = jnp.zeros_like(window)
    centres[...] = jnp.zeros_like(centres)
    for i in range(pos_ref.shape[1] // LANES):
        centres[i, 0:3, :] = pos_ref[:, i * LANES : (i + 1) * LANES]
    last = pos_ref.shape[1] // LANES - 1
    depth = lax.broadcasted_iota(jnp.int32, (2 * LANES, LANES), 0)

    @pl.loop(0, slots)
    def _(s):
        q = s // capacity
        tile = q * tiles + send_ref[q, lax.rem(s, capacity), me]
        atoms = atom_ref[pl.ds(tile, 1), :]
        block = jnp.min(atoms) // LANES
        after = jnp.minimum(block + 1, last)
        window[:, 0:LANES] = centres[block]
        window[:, LANES:] = centres[after]
        pick = jnp.where(depth == atoms - block * LANES, 1.0, 0.0)
        slot_info[s, 0:8, :] = jnp.dot(
            window[...], pick, precision=lax.Precision.HIGHEST, preferred_element_type=f32
        )
        slot_info[s, 3:4, :] = -alpha_ref[pl.ds(tile, 1), :]

    for copy in info_copies:
        copy.wait()
    turned = jnp.concatenate(
        [box_info[...], jnp.zeros((LANES - box_info.shape[0], LANES), f32)], axis=0
    ).T
    for j in range(n_col):
        for b in range(boxes):
            for c in range(4):
                k = j * 16 + c * boxes + b
                planes[j * boxes + b, c] = jnp.broadcast_to(turned[:, k : k + 1], (LANES, LANES))

    def fill(first, count):
        @pl.loop(first, first + count)
        def _(n):
            at = pl.ds(pl.multiple_of(n * LANES, LANES), LANES)

            @pl.loop(0, slots)
            def _(s):
                one = planes[n, 0] - slot_info[s, 0:1, :]
                dist = one * one
                two = planes[n, 1] - slot_info[s, 1:2, :]
                dist = dist + two * two
                three = planes[n, 2] - slot_info[s, 2:3, :]
                dist = dist + three * three
                value = jnp.exp(slot_info[s, 3:4, :] * dist)
                value = jnp.where(planes[n, 3, pl.ds(s, 1), :] > 0.0, value, 0.0)
                phi[at, pl.ds(pl.multiple_of(s * LANES, LANES), LANES)] = value.astype(bf16)

    fill(0, FILLS[0])

    own = pl.ds(pl.multiple_of(me * share, share), share)
    total = part_f[own, :]
    for d in range(1, peers):
        sum_copies[d - 1].wait()
        total = total + got1[d].astype(f32)
    scaled_t[own, :] = lax.dot_general(
        total,
        factor_v[...],
        (((1,), (1,)), ((), ())),
        precision=lax.Precision.HIGHEST,
        preferred_element_type=f32,
    ).astype(bf16)
    gather_copies = []
    for d in range(1, peers):
        copy = pltpu.make_async_remote_copy(
            src_ref=scaled_t.at[own],
            dst_ref=scaled_t.at[own],
            send_sem=gather_send.at[d],
            recv_sem=gather_recv.at[d],
            device_id=in_plane(d)[1],
            device_id_type=MESH,
        )
        copy.start()
        gather_copies.append(copy)

    fill(FILLS[0], FILLS[1])

    for copy in gather_copies:
        copy.wait()

    def rotate(before, vectors):
        change = lax.dot_general(
            vectors, scaled_t[...], (((1,), (1,)), ((), ())), preferred_element_type=f32
        )
        return (before.astype(f32) - change).astype(bf16)

    span = capacity * TILE
    tile_copies = []
    here = pl.ds(pl.multiple_of(me * span, span), span)
    for d in list(range(1, peers)) + [0]:
        peer, where = in_plane(d)
        for j in range(capacity):
            tile = send_ref[me, j, peer]
            outbox[d, j * TILE : (j + 1) * TILE, :] = rotate(coeffs_v[tile], refl_v[tile])
        if d == 0:
            arrived[here, :] = outbox[0]
            continue
        copy = pltpu.make_async_remote_copy(
            src_ref=outbox.at[d],
            dst_ref=arrived.at[here],
            send_sem=tile_send.at[d],
            recv_sem=tile_recv.at[d],
            device_id=where,
            device_id_type=MESH,
        )
        copy.start()
        tile_copies.append(copy)

    def emit(i):
        at = pl.ds(pl.multiple_of(i * EMIT, EMIT), EMIT)
        return pltpu.make_async_copy(rot_v.at[at], rot_hbm.at[at], emit_sem.at[i])

    @pl.loop(0, emits)
    def _(i):
        at = pl.ds(pl.multiple_of(i * EMIT, EMIT), EMIT)
        some = pl.ds(i * (EMIT // TILE), EMIT // TILE)
        rot_v[at, :] = rotate(
            coeffs_v[some].reshape(EMIT, width), refl_v[some].reshape(EMIT, refl_v.shape[2])
        )
        emit(i).start()

    done = FILLS[0] + FILLS[1]
    fill(done, n_col * boxes - done)

    for copy in tile_copies:
        copy.wait()

    lanes = lax.broadcasted_iota(jnp.int32, (LANES, LANES), 1)
    dens_copies = []
    for d in list(range(1, n_col)) + [0]:
        peer, where = in_col(d)
        tall = boxes * LANES
        at = pl.ds(pl.multiple_of(peer * tall, tall), tall)
        orbital = jnp.dot(phi[at, :], arrived[...], preferred_element_type=f32)
        summed = jnp.sum(orbital * orbital, axis=1, keepdims=True)
        spread = jnp.zeros((LANES, LANES), f32)
        for b in range(boxes):
            spread = jnp.where(lanes == b, summed[b * LANES : (b + 1) * LANES], spread)
        dens_own[d] = spread.T[0:8, :]
        if d == 0:
            continue
        copy = pltpu.make_async_remote_copy(
            src_ref=dens_own.at[d],
            dst_ref=dens_got.at[d],
            send_sem=dens_send.at[d],
            recv_sem=dens_recv.at[d],
            device_id=where,
            device_id_type=MESH,
        )
        copy.start()
        dens_copies.append(copy)
    total = dens_own[0]
    for d in range(1, n_col):
        dens_copies[d - 1].wait()
        total = total + dens_got[d]
    dens_ref[...] = total[0:boxes, :] * (1.0 / (K * TILE))

    @pl.loop(0, emits)
    def _(i):
        emit(i).wait()


FILLS = (4, 4)


def fits(coeffs, reflectors, atom_pos, point_pos, send_tiles, sizes):
    n_row, n_box, n_col = sizes
    peers = n_row * n_box
    rows, width = coeffs.shape
    boxes = point_pos.shape[1]
    slots = peers * send_tiles.shape[2]
    return (
        width == LANES
        and rows % LOAD == 0
        and rows % EMIT == 0
        and rows * (reflectors.shape[1] + 2 * width) <= 16 << 20
        and reflectors.shape[1] % LANES == 0
        and width % peers == 0
        and (width // peers) % 16 == 0
        and boxes == 4
        and n_col <= 8
        and point_pos.shape[2] == LANES
        and atom_pos.shape[1] % LANES == 0
        and slots <= LANES
        and n_col * boxes * slots <= 512
        and n_col * boxes >= FILLS[0] + FILLS[1]
    )


def per_device(
    coeffs,
    reflectors,
    factor,
    func_exp,
    func_atom,
    atom_pos,
    point_pos,
    send_tiles,
    box_tiles,
    box_count,
):
    sizes = lax.axis_size("row"), lax.axis_size("box"), lax.axis_size("col")
    if not fits(coeffs, reflectors, atom_pos, point_pos, send_tiles, sizes):
        return general(
            coeffs,
            reflectors,
            factor,
            func_exp,
            func_atom,
            atom_pos,
            point_pos,
            send_tiles,
            box_tiles,
            box_count,
        )
    n_row, n_box, n_col = sizes
    peers = n_row * n_box
    rows, width = coeffs.shape
    nref = reflectors.shape[1]
    boxes = point_pos.shape[1]
    capacity = send_tiles.shape[2]
    slots = peers * capacity
    f32, bf16 = jnp.float32, jnp.bfloat16
    vmem = pl.BlockSpec(memory_space=pltpu.VMEM)
    smem = pl.BlockSpec(memory_space=pltpu.SMEM)
    hbm = pl.BlockSpec(memory_space=pltpu.HBM)
    anywhere = pl.BlockSpec(memory_space=pl.ANY)
    dma = pltpu.SemaphoreType.DMA
    rotated, density = pl.pallas_call(
        functools.partial(kernel, n_row, n_box, n_col),
        out_shape=(
            jax.ShapeDtypeStruct((rows, width), bf16),
            jax.ShapeDtypeStruct((boxes, LANES), f32),
        ),
        in_specs=[hbm] * 6 + [vmem, smem, smem, smem],
        out_specs=(anywhere, vmem),
        scratch_shapes=[
            pltpu.VMEM((rows // TILE, TILE, width), bf16),
            pltpu.VMEM((rows // TILE, TILE, nref), bf16),
            pltpu.VMEM((rows, width), bf16),
            pltpu.VMEM((width, nref), f32),
            pltpu.VMEM((width, nref), bf16),
            pltpu.VMEM((peers, width // peers, nref), bf16),
            pltpu.VMEM((width, nref), bf16),
            pltpu.VMEM((peers, capacity * TILE, width), bf16),
            pltpu.VMEM((slots * TILE, width), bf16),
            pltpu.VMEM((n_col * 16, LANES), f32),
            pltpu.VMEM((n_col * boxes, 4, LANES, LANES), f32),
            pltpu.VMEM((8, 2 * LANES), f32),
            pltpu.VMEM((slots, 8, LANES), f32),
            pltpu.VMEM((n_col * boxes * LANES, slots * TILE), bf16),
            pltpu.VMEM((n_col, 8, LANES), f32),
            pltpu.VMEM((n_col, 8, LANES), f32),
            pltpu.VMEM(factor.shape, f32),
            pltpu.VMEM((func_exp.shape[0] // TILE, TILE), f32),
            pltpu.VMEM((func_exp.shape[0] // TILE, TILE), jnp.int32),
            pltpu.VMEM(atom_pos.shape, f32),
            pltpu.VMEM((atom_pos.shape[1] // LANES, 8, LANES), f32),
            dma((4,)),
            dma((2 * (rows // LOAD),)),
            dma((rows // EMIT,)),
            dma((n_col,)),
            dma((n_col,)),
            dma((peers,)),
            dma((peers,)),
            dma((peers,)),
            dma((peers,)),
            dma((peers,)),
            dma((peers,)),
            dma((n_col,)),
            dma((n_col,)),
        ],
        compiler_params=pltpu.CompilerParams(
            collective_id=0, has_side_effects=True, vmem_limit_bytes=63 << 20
        ),
        name="panel_and_density",
    )(
        coeffs.reshape(-1, TILE, width),
        reflectors.reshape(-1, TILE, nref),
        factor,
        func_exp.reshape(-1, TILE),
        func_atom.reshape(-1, TILE),
        atom_pos,
        point_pos,
        jnp.swapaxes(send_tiles, 1, 2),
        box_tiles,
        box_count,
    )
    return rotated, density


def solution(mesh):
    in_specs = (
        P(("row", "box"), "col"),
        P(("row", "box"), None),
        P(),
        P(),
        P(),
        P(),
        P(None, ("row", "col", "box"), None),
        P(),
        P(("row", "col", "box"), None),
        P(("row", "col", "box")),
    )
    out_specs = (P(("row", "box"), "col"), P(("row", "col", "box"), None))
    return jax.shard_map(
        per_device, mesh=mesh, in_specs=in_specs, out_specs=out_specs, check_vma=False
    )
```

```python
import functools
import math

import jax
import jax.numpy as jnp
from jax import lax
from jax.experimental import pallas as pl
from jax.experimental.pallas import tpu as pltpu
from jax.sharding import PartitionSpec as P

K = 512
TILE = 128


def box_density(arrived, slot_alpha, slot_centre, listed, count, points):
    alpha = slot_alpha[listed]
    centre = slot_centre[:, listed]
    first = points[0][:, None, None] - centre[0][None]
    dist = first * first
    second = points[1][:, None, None] - centre[1][None]
    dist = dist + second * second
    third = points[2][:, None, None] - centre[2][None]
    dist = dist + third * third
    live = jnp.arange(listed.shape[0], dtype=jnp.int32) < count
    phi = jnp.where(live[None, :, None], jnp.exp(-alpha[None] * dist), 0.0).astype(jnp.bfloat16)
    phi = phi.reshape(points.shape[1], -1)
    block = arrived[listed].reshape(-1, arrived.shape[2])
    orbital = jnp.dot(phi, block, preferred_element_type=jnp.float32)
    return jnp.sum(orbital * orbital, 1) / (K * TILE)


def by_blocks(arrived, slot_alpha, slot_centre, lists, counts, points):
    boxes = lists.shape[0]
    width = math.gcd(boxes, 2)
    steps = boxes // width
    lists_blocked = lists.reshape(steps, width, lists.shape[1])
    counts_blocked = counts.reshape(steps, width)
    moved = jnp.moveaxis(points, 1, 0)
    points_blocked = moved.reshape(steps, width, moved.shape[1], moved.shape[2])
    single = jax.vmap(
        lambda listed, count, where: box_density(
            arrived, slot_alpha, slot_centre, listed, count, where
        )
    )

    def one_block(items):
        return single(items[0], items[1], items[2])

    result = lax.map(one_block, (lists_blocked, counts_blocked, points_blocked))
    return result.reshape(boxes, result.shape[2])


def general(
    coeffs,
    reflectors,
    factor,
    func_exp,
    func_atom,
    atom_pos,
    point_pos,
    send_tiles,
    box_tiles,
    box_count,
):
    panel_part = jnp.dot(reflectors.T, coeffs, preferred_element_type=jnp.float32)
    panel = lax.psum(panel_part.astype(jnp.bfloat16), ("row", "box")).astype(jnp.float32)
    scaled = jnp.dot(factor, panel, precision=lax.Precision.HIGHEST).astype(jnp.bfloat16)
    rotated = (
        coeffs.astype(jnp.float32) - jnp.dot(reflectors, scaled, preferred_element_type=jnp.float32)
    ).astype(jnp.bfloat16)
    peers = lax.axis_size(("row", "box"))
    group = lax.axis_index(("row", "box"))
    capacity = send_tiles.shape[2]
    local_tiles = coeffs.shape[0] // TILE
    slots = jnp.arange(peers * capacity, dtype=jnp.int32)
    source = slots // capacity
    within = slots % capacity
    tile = source * local_tiles + send_tiles[source, group, within]
    funcs = tile[:, None] * TILE + jnp.arange(TILE, dtype=jnp.int32)[None, :]
    slot_alpha = func_exp[funcs]
    slot_centre = atom_pos[:, func_atom[funcs]]
    outgoing_index = send_tiles[group]
    outgoing = rotated.reshape(local_tiles, TILE, rotated.shape[1])[outgoing_index]
    arrived = lax.all_to_all(outgoing, ("row", "box"), split_axis=0, concat_axis=0, tiled=True)
    arrived = arrived.reshape(peers * capacity, TILE, arrived.shape[3])
    lists, counts = (
        lax.all_gather(box_tiles, "col", axis=0, tiled=True),
        lax.all_gather(box_count, "col", axis=0, tiled=True),
    )
    points = lax.all_gather(point_pos, "col", axis=1, tiled=True)
    partial_value = by_blocks(arrived, slot_alpha, slot_centre, lists, counts, points)
    density = lax.psum_scatter(
        partial_value.astype(jnp.bfloat16), "col", scatter_dimension=0, tiled=True
    ).astype(jnp.float32)
    return (rotated, density)


MESH = pl.DeviceIdType.MESH
LANES = 128
LOAD = 1024
EMIT = 1024


def kernel(
    n_row,
    n_box,
    n_col,
    coeffs_hbm,
    refl_hbm,
    factor_hbm,
    alpha_hbm,
    atom_hbm,
    pos_hbm,
    point_ref,
    send_ref,
    list_ref,
    count_ref,
    rot_hbm,
    dens_ref,
    coeffs_v,
    refl_v,
    rot_v,
    part_f,
    part_b,
    got1,
    scaled_t,
    outbox,
    arrived,
    box_info,
    planes,
    window,
    slot_info,
    phi,
    dens_own,
    dens_got,
    orbitals,
    factor_v,
    alpha_ref,
    atom_ref,
    pos_ref,
    centres,
    table_sem,
    load_sem,
    emit_sem,
    info_send,
    info_recv,
    sum_send,
    sum_recv,
    gather_send,
    gather_recv,
    tile_send,
    tile_recv,
    dens_send,
    dens_recv,
):
    f32, bf16 = jnp.float32, jnp.bfloat16
    peers = n_row * n_box
    row, box, col = lax.axis_index("row"), lax.axis_index("box"), lax.axis_index("col")
    me = row * n_box + box
    tiles, _, width = coeffs_v.shape
    rows = tiles * TILE
    loads = rows // LOAD
    emits = rows // EMIT
    share = width // peers
    slots, capacity = slot_info.shape[0], send_ref.shape[1]
    boxes = dens_ref.shape[0]
    step = LOAD // TILE

    def load(i):
        at = pl.ds(i * step, step)
        return (
            pltpu.make_async_copy(coeffs_hbm.at[at], coeffs_v.at[at], load_sem.at[2 * i]),
            pltpu.make_async_copy(refl_hbm.at[at], refl_v.at[at], load_sem.at[2 * i + 1]),
        )

    for i in range(loads):
        for copy in load(i):
            copy.start()

    tables = [
        pltpu.make_async_copy(source, target, table_sem.at[i])
        for i, (source, target) in enumerate(
            [
                (atom_hbm, atom_ref),
                (alpha_hbm, alpha_ref),
                (pos_hbm, pos_ref),
                (factor_hbm, factor_v),
            ]
        )
    ]
    for copy in tables:
        copy.start()

    def in_plane(d):
        peer = lax.rem(me + d, peers)
        return peer, {"row": peer // n_box, "box": lax.rem(peer, n_box)}

    def in_col(d):
        peer = lax.rem(col + d, n_col)
        return peer, {"col": peer}

    barrier = pltpu.get_barrier_semaphore()
    for d in range(1, peers):
        pl.semaphore_signal(barrier, inc=1, device_id=in_plane(d)[1], device_id_type=MESH)
    for d in range(1, n_col):
        pl.semaphore_signal(barrier, inc=1, device_id=in_col(d)[1], device_id_type=MESH)

    mine = pl.ds(pl.multiple_of(col * 16, 16), 16)
    lane = lax.broadcasted_iota(jnp.int32, (1, LANES), 1)
    info = [point_ref[c] for c in range(3)]
    for b in range(boxes):
        live = jnp.zeros((1, LANES), f32)
        for i in range(list_ref.shape[1]):
            used = jnp.where(i < count_ref[b], list_ref[b, i], -1)
            live = jnp.where(lane == used, 1.0, live)
        info.append(live)
    box_info[mine, :] = jnp.concatenate(info, axis=0)

    for copy in tables:
        copy.wait()
    centres[...] = jnp.zeros_like(centres)
    for i in range(pos_ref.shape[1] // LANES):
        centres[i, 0:3, :] = pos_ref[:, i * LANES : (i + 1) * LANES]
    last = pos_ref.shape[1] // LANES - 1
    depth = lax.broadcasted_iota(jnp.int32, (2 * LANES, LANES), 0)

    for s in range(slots):
        q = s // capacity
        tile = q * tiles + send_ref[q, s % capacity, me]
        atoms = atom_ref[pl.ds(tile, 1), :]
        block = jnp.min(atoms) // LANES
        after = jnp.minimum(block + 1, last)
        window[s, :, 0:LANES] = centres[block]
        window[s, :, LANES:] = centres[after]
        pick = jnp.where(depth == atoms - block * LANES, 1.0, 0.0).astype(bf16)
        whole = window[s]
        high = whole.astype(bf16).astype(f32)
        middle = (whole - high).astype(bf16).astype(f32)
        split = jnp.concatenate([high, middle, whole - high - middle], axis=0).astype(bf16)
        three = jnp.dot(split, pick, preferred_element_type=f32)
        slot_info[s, 0:8, :] = three[0:8] + three[8:16] + three[16:24]
        slot_info[s, 3:4, :] = -alpha_ref[pl.ds(tile, 1), :]

    part_f[...] = jnp.zeros_like(part_f)

    @pl.loop(0, loads)
    def _(i):
        for copy in load(i):
            copy.wait()
        at = pl.ds(i * step, step)
        part_f[...] += lax.dot_general(
            coeffs_v[at].reshape(LOAD, width),
            refl_v[at].reshape(LOAD, refl_v.shape[2]),
            (((0,), (0,)), ((), ())),
            preferred_element_type=f32,
        )

    pl.semaphore_wait(barrier, peers - 1 + n_col - 1)

    part_b[...] = part_f[...].astype(bf16)
    sum_copies = []
    for d in range(1, peers):
        peer, where = in_plane(d)
        copy = pltpu.make_async_remote_copy(
            src_ref=part_b.at[pl.ds(pl.multiple_of(peer * share, share), share)],
            dst_ref=got1.at[d],
            send_sem=sum_send.at[d],
            recv_sem=sum_recv.at[d],
            device_id=where,
            device_id_type=MESH,
        )
        copy.start()
        sum_copies.append(copy)

    info_copies = []
    for d in range(1, n_col):
        copy = pltpu.make_async_remote_copy(
            src_ref=box_info.at[mine],
            dst_ref=box_info.at[mine],
            send_sem=info_send.at[d],
            recv_sem=info_recv.at[d],
            device_id=in_col(d)[1],
            device_id_type=MESH,
        )
        copy.start()
        info_copies.append(copy)

    def spread(j, block):
        for b in range(boxes):
            for c in range(4):
                k = c * boxes + b
                planes[j * boxes + b, c] = jnp.broadcast_to(block[:, k : k + 1], (LANES, LANES))

    def turn(j):
        at = pl.ds(pl.multiple_of(j * 16, 16), 16)
        return jnp.concatenate([box_info[at, :], jnp.zeros((LANES - 16, LANES), f32)], axis=0).T

    spread(col, turn(col))

    def fill(first, count):
        @pl.loop(first, first + count)
        def _(n):
            at = pl.ds(pl.multiple_of(n * LANES, LANES), LANES)

            @pl.loop(0, slots)
            def _(s):
                one = planes[n, 0] - slot_info[s, 0:1, :]
                dist = one * one
                two = planes[n, 1] - slot_info[s, 1:2, :]
                dist = dist + two * two
                three = planes[n, 2] - slot_info[s, 2:3, :]
                dist = dist + three * three
                value = jnp.exp(slot_info[s, 3:4, :] * dist)
                value = jnp.where(planes[n, 3, pl.ds(s, 1), :] > 0.0, value, 0.0)
                phi[at, pl.ds(pl.multiple_of(s * LANES, LANES), LANES)] = value.astype(bf16)

    fill(col * boxes, boxes)

    own = pl.ds(pl.multiple_of(me * share, share), share)
    total = part_f[own, :]
    for d in range(1, peers):
        sum_copies[d - 1].wait()
        total = total + got1[d].astype(f32)
    scaled_t[own, :] = lax.dot_general(
        total,
        factor_v[...],
        (((1,), (1,)), ((), ())),
        precision=lax.Precision.HIGHEST,
        preferred_element_type=f32,
    ).astype(bf16)
    gather_copies = []
    for d in range(1, peers):
        copy = pltpu.make_async_remote_copy(
            src_ref=scaled_t.at[own],
            dst_ref=scaled_t.at[own],
            send_sem=gather_send.at[d],
            recv_sem=gather_recv.at[d],
            device_id=in_plane(d)[1],
            device_id_type=MESH,
        )
        copy.start()
        gather_copies.append(copy)

    def fill_col(d):
        info_copies[d - 1].wait()
        peer = lax.rem(col + n_col - d, n_col)
        spread(peer, turn(peer))
        fill(peer * boxes, boxes)

    fill_col(1)

    for copy in gather_copies:
        copy.wait()

    def rotate(before, vectors):
        change = lax.dot_general(
            vectors, scaled_t[...], (((1,), (1,)), ((), ())), preferred_element_type=f32
        )
        return (before.astype(f32) - change).astype(bf16)

    span = capacity * TILE
    tile_copies = []
    here = pl.ds(pl.multiple_of(me * span, span), span)
    for d in list(range(1, peers)) + [0]:
        peer, where = in_plane(d)
        for j in range(capacity):
            tile = send_ref[me, j, peer]
            outbox[d, j * TILE : (j + 1) * TILE, :] = rotate(coeffs_v[tile], refl_v[tile])
        if d == 0:
            arrived[here, :] = outbox[0]
            continue
        copy = pltpu.make_async_remote_copy(
            src_ref=outbox.at[d],
            dst_ref=arrived.at[here],
            send_sem=tile_send.at[d],
            recv_sem=tile_recv.at[d],
            device_id=where,
            device_id_type=MESH,
        )
        copy.start()
        tile_copies.append(copy)

    def emit(i):
        at = pl.ds(pl.multiple_of(i * EMIT, EMIT), EMIT)
        return pltpu.make_async_copy(rot_v.at[at], rot_hbm.at[at], emit_sem.at[i])

    @pl.loop(0, emits)
    def _(i):
        at = pl.ds(pl.multiple_of(i * EMIT, EMIT), EMIT)
        some = pl.ds(i * (EMIT // TILE), EMIT // TILE)
        rot_v[at, :] = rotate(
            coeffs_v[some].reshape(EMIT, width), refl_v[some].reshape(EMIT, refl_v.shape[2])
        )
        emit(i).start()

    for d in range(2, n_col):
        fill_col(d)

    def add(q, first):
        deep = pl.ds(pl.multiple_of(q * span, span), span)

        @pl.loop(0, n_col)
        def _(j):
            at = pl.ds(pl.multiple_of(j * boxes * LANES, LANES), boxes * LANES)
            part = jnp.dot(phi[at, deep], arrived[deep, :], preferred_element_type=f32)
            orbitals[at, :] = part if first else orbitals[at, :] + part

    add(me, True)
    for d in range(1, peers):
        tile_copies[d - 1].wait()
        add(lax.rem(me + peers - d, peers), False)

    lanes = lax.broadcasted_iota(jnp.int32, (LANES, LANES), 1)
    dens_copies = []
    for d in list(range(1, n_col)) + [0]:
        peer, where = in_col(d)
        tall = boxes * LANES
        at = pl.ds(pl.multiple_of(peer * tall, tall), tall)
        orbital = orbitals[at, :]
        summed = jnp.sum(orbital * orbital, axis=1, keepdims=True)
        turned = jnp.zeros((LANES, LANES), f32)
        for b in range(boxes):
            turned = jnp.where(lanes == b, summed[b * LANES : (b + 1) * LANES], turned)
        dens_own[d] = turned.T[0:8, :]
        if d == 0:
            continue
        copy = pltpu.make_async_remote_copy(
            src_ref=dens_own.at[d],
            dst_ref=dens_got.at[d],
            send_sem=dens_send.at[d],
            recv_sem=dens_recv.at[d],
            device_id=where,
            device_id_type=MESH,
        )
        copy.start()
        dens_copies.append(copy)
    total = dens_own[0]
    for d in range(1, n_col):
        dens_copies[d - 1].wait()
        total = total + dens_got[d]
    dens_ref[...] = total[0:boxes, :] * (1.0 / (K * TILE))

    @pl.loop(0, emits)
    def _(i):
        emit(i).wait()


def fits(coeffs, reflectors, atom_pos, point_pos, send_tiles, sizes):
    n_row, n_box, n_col = sizes
    peers = n_row * n_box
    rows, width = coeffs.shape
    boxes = point_pos.shape[1]
    slots = peers * send_tiles.shape[2]
    return (
        width == LANES
        and rows % LOAD == 0
        and rows % EMIT == 0
        and rows * (reflectors.shape[1] + 2 * width) <= 16 << 20
        and reflectors.shape[1] % LANES == 0
        and width % peers == 0
        and (width // peers) % 16 == 0
        and boxes == 4
        and n_col <= 8
        and point_pos.shape[2] == LANES
        and atom_pos.shape[1] % LANES == 0
        and slots <= LANES
        and n_col * boxes * slots <= 512
        and n_col >= 2
    )


def per_device(
    coeffs,
    reflectors,
    factor,
    func_exp,
    func_atom,
    atom_pos,
    point_pos,
    send_tiles,
    box_tiles,
    box_count,
):
    sizes = lax.axis_size("row"), lax.axis_size("box"), lax.axis_size("col")
    if not fits(coeffs, reflectors, atom_pos, point_pos, send_tiles, sizes):
        return general(
            coeffs,
            reflectors,
            factor,
            func_exp,
            func_atom,
            atom_pos,
            point_pos,
            send_tiles,
            box_tiles,
            box_count,
        )
    n_row, n_box, n_col = sizes
    peers = n_row * n_box
    rows, width = coeffs.shape
    nref = reflectors.shape[1]
    boxes = point_pos.shape[1]
    capacity = send_tiles.shape[2]
    slots = peers * capacity
    f32, bf16 = jnp.float32, jnp.bfloat16
    vmem = pl.BlockSpec(memory_space=pltpu.VMEM)
    smem = pl.BlockSpec(memory_space=pltpu.SMEM)
    hbm = pl.BlockSpec(memory_space=pltpu.HBM)
    anywhere = pl.BlockSpec(memory_space=pl.ANY)
    dma = pltpu.SemaphoreType.DMA
    rotated, density = pl.pallas_call(
        functools.partial(kernel, n_row, n_box, n_col),
        out_shape=(
            jax.ShapeDtypeStruct((rows, width), bf16),
            jax.ShapeDtypeStruct((boxes, LANES), f32),
        ),
        in_specs=[hbm] * 6 + [vmem, smem, smem, smem],
        out_specs=(anywhere, vmem),
        scratch_shapes=[
            pltpu.VMEM((rows // TILE, TILE, width), bf16),
            pltpu.VMEM((rows // TILE, TILE, nref), bf16),
            pltpu.VMEM((rows, width), bf16),
            pltpu.VMEM((width, nref), f32),
            pltpu.VMEM((width, nref), bf16),
            pltpu.VMEM((peers, width // peers, nref), bf16),
            pltpu.VMEM((width, nref), bf16),
            pltpu.VMEM((peers, capacity * TILE, width), bf16),
            pltpu.VMEM((slots * TILE, width), bf16),
            pltpu.VMEM((n_col * 16, LANES), f32),
            pltpu.VMEM((n_col * boxes, 4, LANES, LANES), f32),
            pltpu.VMEM((slots, 8, 2 * LANES), f32),
            pltpu.VMEM((slots, 8, LANES), f32),
            pltpu.VMEM((n_col * boxes * LANES, slots * TILE), bf16),
            pltpu.VMEM((n_col, 8, LANES), f32),
            pltpu.VMEM((n_col, 8, LANES), f32),
            pltpu.VMEM((n_col * boxes * LANES, width), f32),
            pltpu.VMEM(factor.shape, f32),
            pltpu.VMEM((func_exp.shape[0] // TILE, TILE), f32),
            pltpu.VMEM((func_exp.shape[0] // TILE, TILE), jnp.int32),
            pltpu.VMEM(atom_pos.shape, f32),
            pltpu.VMEM((atom_pos.shape[1] // LANES, 8, LANES), f32),
            dma((4,)),
            dma((2 * (rows // LOAD),)),
            dma((rows // EMIT,)),
            dma((n_col,)),
            dma((n_col,)),
            dma((peers,)),
            dma((peers,)),
            dma((peers,)),
            dma((peers,)),
            dma((peers,)),
            dma((peers,)),
            dma((n_col,)),
            dma((n_col,)),
        ],
        compiler_params=pltpu.CompilerParams(
            collective_id=0, has_side_effects=True, vmem_limit_bytes=63 << 20
        ),
        name="panel_and_density",
    )(
        coeffs.reshape(-1, TILE, width),
        reflectors.reshape(-1, TILE, nref),
        factor,
        func_exp.reshape(-1, TILE),
        func_atom.reshape(-1, TILE),
        atom_pos,
        point_pos,
        jnp.swapaxes(send_tiles, 1, 2),
        box_tiles,
        box_count,
    )
    return rotated, density


def solution(mesh):
    in_specs = (
        P(("row", "box"), "col"),
        P(("row", "box"), None),
        P(),
        P(),
        P(),
        P(),
        P(None, ("row", "col", "box"), None),
        P(),
        P(("row", "col", "box"), None),
        P(("row", "col", "box")),
    )
    out_specs = (P(("row", "box"), "col"), P(("row", "col", "box"), None))
    return jax.shard_map(
        per_device, mesh=mesh, in_specs=in_specs, out_specs=out_specs, check_vma=False
    )
```

```python
import functools
import math

import jax
import jax.numpy as jnp
from jax import lax
from jax.experimental import pallas as pl
from jax.experimental.pallas import tpu as pltpu
from jax.sharding import PartitionSpec as P

K = 512
TILE = 128


def box_density(arrived, slot_alpha, slot_centre, listed, count, points):
    alpha = slot_alpha[listed]
    centre = slot_centre[:, listed]
    first = points[0][:, None, None] - centre[0][None]
    dist = first * first
    second = points[1][:, None, None] - centre[1][None]
    dist = dist + second * second
    third = points[2][:, None, None] - centre[2][None]
    dist = dist + third * third
    live = jnp.arange(listed.shape[0], dtype=jnp.int32) < count
    phi = jnp.where(live[None, :, None], jnp.exp(-alpha[None] * dist), 0.0).astype(jnp.bfloat16)
    phi = phi.reshape(points.shape[1], -1)
    block = arrived[listed].reshape(-1, arrived.shape[2])
    orbital = jnp.dot(phi, block, preferred_element_type=jnp.float32)
    return jnp.sum(orbital * orbital, 1) / (K * TILE)


def by_blocks(arrived, slot_alpha, slot_centre, lists, counts, points):
    boxes = lists.shape[0]
    width = math.gcd(boxes, 2)
    steps = boxes // width
    lists_blocked = lists.reshape(steps, width, lists.shape[1])
    counts_blocked = counts.reshape(steps, width)
    moved = jnp.moveaxis(points, 1, 0)
    points_blocked = moved.reshape(steps, width, moved.shape[1], moved.shape[2])
    single = jax.vmap(
        lambda listed, count, where: box_density(
            arrived, slot_alpha, slot_centre, listed, count, where
        )
    )

    def one_block(items):
        return single(items[0], items[1], items[2])

    result = lax.map(one_block, (lists_blocked, counts_blocked, points_blocked))
    return result.reshape(boxes, result.shape[2])


def general(
    coeffs,
    reflectors,
    factor,
    func_exp,
    func_atom,
    atom_pos,
    point_pos,
    send_tiles,
    box_tiles,
    box_count,
):
    panel_part = jnp.dot(reflectors.T, coeffs, preferred_element_type=jnp.float32)
    panel = lax.psum(panel_part.astype(jnp.bfloat16), ("row", "box")).astype(jnp.float32)
    scaled = jnp.dot(factor, panel, precision=lax.Precision.HIGHEST).astype(jnp.bfloat16)
    rotated = (
        coeffs.astype(jnp.float32) - jnp.dot(reflectors, scaled, preferred_element_type=jnp.float32)
    ).astype(jnp.bfloat16)
    peers = lax.axis_size(("row", "box"))
    group = lax.axis_index(("row", "box"))
    capacity = send_tiles.shape[2]
    local_tiles = coeffs.shape[0] // TILE
    slots = jnp.arange(peers * capacity, dtype=jnp.int32)
    source = slots // capacity
    within = slots % capacity
    tile = source * local_tiles + send_tiles[source, group, within]
    funcs = tile[:, None] * TILE + jnp.arange(TILE, dtype=jnp.int32)[None, :]
    slot_alpha = func_exp[funcs]
    slot_centre = atom_pos[:, func_atom[funcs]]
    outgoing_index = send_tiles[group]
    outgoing = rotated.reshape(local_tiles, TILE, rotated.shape[1])[outgoing_index]
    arrived = lax.all_to_all(outgoing, ("row", "box"), split_axis=0, concat_axis=0, tiled=True)
    arrived = arrived.reshape(peers * capacity, TILE, arrived.shape[3])
    lists, counts = (
        lax.all_gather(box_tiles, "col", axis=0, tiled=True),
        lax.all_gather(box_count, "col", axis=0, tiled=True),
    )
    points = lax.all_gather(point_pos, "col", axis=1, tiled=True)
    partial_value = by_blocks(arrived, slot_alpha, slot_centre, lists, counts, points)
    density = lax.psum_scatter(
        partial_value.astype(jnp.bfloat16), "col", scatter_dimension=0, tiled=True
    ).astype(jnp.float32)
    return (rotated, density)


MESH = pl.DeviceIdType.MESH
LANES = 128
LOAD = 1024
EMIT = 1024


def kernel(
    n_row,
    n_box,
    n_col,
    coeffs_hbm,
    refl_hbm,
    factor_hbm,
    alpha_hbm,
    atom_hbm,
    pos_hbm,
    point_hbm,
    send_hbm,
    list_hbm,
    count_hbm,
    rot_hbm,
    dens_ref,
    coeffs_v,
    refl_v,
    rot_v,
    part_f,
    part_b,
    got1,
    scaled_t,
    outbox,
    arrived,
    box_info,
    planes,
    window,
    slot_info,
    phi,
    dens_own,
    dens_got,
    point_ref,
    send_ref,
    list_ref,
    count_ref,
    orbitals,
    factor_v,
    alpha_ref,
    atom_ref,
    pos_ref,
    centres,
    table_sem,
    load_sem,
    emit_sem,
    info_send,
    info_recv,
    sum_send,
    sum_recv,
    gather_send,
    gather_recv,
    tile_send,
    tile_recv,
    dens_send,
    dens_recv,
):
    f32, bf16 = jnp.float32, jnp.bfloat16
    peers = n_row * n_box
    row, box, col = lax.axis_index("row"), lax.axis_index("box"), lax.axis_index("col")
    me = row * n_box + box
    tiles, _, width = coeffs_v.shape
    rows = tiles * TILE
    loads = rows // LOAD
    emits = rows // EMIT
    share = width // peers
    slots, capacity = slot_info.shape[0], send_ref.shape[1]
    boxes = dens_ref.shape[0]
    step = LOAD // TILE

    def load(i):
        at = pl.ds(i * step, step)
        return (
            pltpu.make_async_copy(coeffs_hbm.at[at], coeffs_v.at[at], load_sem.at[2 * i]),
            pltpu.make_async_copy(refl_hbm.at[at], refl_v.at[at], load_sem.at[2 * i + 1]),
        )

    for i in range(loads):
        for copy in load(i):
            copy.start()

    tables = [
        pltpu.make_async_copy(source, target, table_sem.at[i])
        for i, (source, target) in enumerate(
            [
                (point_hbm, point_ref),
                (list_hbm, list_ref),
                (count_hbm, count_ref),
                (send_hbm, send_ref),
                (atom_hbm, atom_ref),
                (alpha_hbm, alpha_ref),
                (pos_hbm, pos_ref),
                (factor_hbm, factor_v),
            ]
        )
    ]
    for copy in tables:
        copy.start()

    def in_plane(d):
        peer = lax.rem(me + d, peers)
        return peer, {"row": peer // n_box, "box": lax.rem(peer, n_box)}

    def in_col(d):
        peer = lax.rem(col + d, n_col)
        return peer, {"col": peer}

    barrier = pltpu.get_barrier_semaphore()
    for d in range(1, peers):
        pl.semaphore_signal(barrier, inc=1, device_id=in_plane(d)[1], device_id_type=MESH)
    for d in range(1, n_col):
        pl.semaphore_signal(barrier, inc=1, device_id=in_col(d)[1], device_id_type=MESH)

    for copy in tables[:3]:
        copy.wait()
    mine = pl.ds(pl.multiple_of(col * 16, 16), 16)
    lane = lax.broadcasted_iota(jnp.int32, (1, LANES), 1)
    info = [point_ref[c] for c in range(3)]
    for b in range(boxes):
        live = jnp.zeros((1, LANES), f32)
        for i in range(list_ref.shape[1]):
            used = jnp.where(i < count_ref[b], list_ref[b, i], -1)
            live = jnp.where(lane == used, 1.0, live)
        info.append(live)
    box_info[mine, :] = jnp.concatenate(info, axis=0)

    for copy in tables[3:]:
        copy.wait()
    centres[...] = jnp.zeros_like(centres)
    for i in range(pos_ref.shape[1] // LANES):
        centres[i, 0:3, :] = pos_ref[:, i * LANES : (i + 1) * LANES]
    last = pos_ref.shape[1] // LANES - 1
    depth = lax.broadcasted_iota(jnp.int32, (2 * LANES, LANES), 0)

    for s in range(slots):
        q = s // capacity
        tile = q * tiles + send_ref[q, s % capacity, me]
        atoms = atom_ref[pl.ds(tile, 1), :]
        block = jnp.min(atoms) // LANES
        after = jnp.minimum(block + 1, last)
        window[s, :, 0:LANES] = centres[block]
        window[s, :, LANES:] = centres[after]
        pick = jnp.where(depth == atoms - block * LANES, 1.0, 0.0).astype(bf16)
        whole = window[s]
        high = whole.astype(bf16).astype(f32)
        middle = (whole - high).astype(bf16).astype(f32)
        split = jnp.concatenate([high, middle, whole - high - middle], axis=0).astype(bf16)
        three = jnp.dot(split, pick, preferred_element_type=f32)
        slot_info[s, 0:8, :] = three[0:8] + three[8:16] + three[16:24]
        slot_info[s, 3:4, :] = -alpha_ref[pl.ds(tile, 1), :]

    part_f[...] = jnp.zeros_like(part_f)

    @pl.loop(0, loads)
    def _(i):
        for copy in load(i):
            copy.wait()
        at = pl.ds(i * step, step)
        part_f[...] += lax.dot_general(
            coeffs_v[at].reshape(LOAD, width),
            refl_v[at].reshape(LOAD, refl_v.shape[2]),
            (((0,), (0,)), ((), ())),
            preferred_element_type=f32,
        )

    pl.semaphore_wait(barrier, peers - 1 + n_col - 1)

    part_b[...] = part_f[...].astype(bf16)
    sum_copies = []
    for d in range(1, peers):
        peer, where = in_plane(d)
        copy = pltpu.make_async_remote_copy(
            src_ref=part_b.at[pl.ds(pl.multiple_of(peer * share, share), share)],
            dst_ref=got1.at[d],
            send_sem=sum_send.at[d],
            recv_sem=sum_recv.at[d],
            device_id=where,
            device_id_type=MESH,
        )
        copy.start()
        sum_copies.append(copy)

    info_copies = []
    for d in range(1, n_col):
        copy = pltpu.make_async_remote_copy(
            src_ref=box_info.at[mine],
            dst_ref=box_info.at[mine],
            send_sem=info_send.at[d],
            recv_sem=info_recv.at[d],
            device_id=in_col(d)[1],
            device_id_type=MESH,
        )
        copy.start()
        info_copies.append(copy)

    def spread(j, block):
        for b in range(boxes):
            for c in range(4):
                k = c * boxes + b
                planes[j * boxes + b, c] = jnp.broadcast_to(block[:, k : k + 1], (LANES, LANES))

    def turn(j):
        at = pl.ds(pl.multiple_of(j * 16, 16), 16)
        return jnp.concatenate([box_info[at, :], jnp.zeros((LANES - 16, LANES), f32)], axis=0).T

    spread(col, turn(col))

    def fill(first, count):
        @pl.loop(first, first + count)
        def _(n):
            at = pl.ds(pl.multiple_of(n * LANES, LANES), LANES)

            @pl.loop(0, slots)
            def _(s):
                one = planes[n, 0] - slot_info[s, 0:1, :]
                dist = one * one
                two = planes[n, 1] - slot_info[s, 1:2, :]
                dist = dist + two * two
                three = planes[n, 2] - slot_info[s, 2:3, :]
                dist = dist + three * three
                value = jnp.exp(slot_info[s, 3:4, :] * dist)
                value = jnp.where(planes[n, 3, pl.ds(s, 1), :] > 0.0, value, 0.0)
                phi[at, pl.ds(pl.multiple_of(s * LANES, LANES), LANES)] = value.astype(bf16)

    fill(col * boxes, boxes)

    own = pl.ds(pl.multiple_of(me * share, share), share)
    total = part_f[own, :]
    for d in range(1, peers):
        sum_copies[d - 1].wait()
        total = total + got1[d].astype(f32)
    scaled_t[own, :] = lax.dot_general(
        total,
        factor_v[...],
        (((1,), (1,)), ((), ())),
        precision=lax.Precision.HIGHEST,
        preferred_element_type=f32,
    ).astype(bf16)
    gather_copies = []
    for d in range(1, peers):
        copy = pltpu.make_async_remote_copy(
            src_ref=scaled_t.at[own],
            dst_ref=scaled_t.at[own],
            send_sem=gather_send.at[d],
            recv_sem=gather_recv.at[d],
            device_id=in_plane(d)[1],
            device_id_type=MESH,
        )
        copy.start()
        gather_copies.append(copy)

    def fill_col(d):
        info_copies[d - 1].wait()
        peer = lax.rem(col + n_col - d, n_col)
        spread(peer, turn(peer))
        fill(peer * boxes, boxes)

    fill_col(1)

    for copy in gather_copies:
        copy.wait()

    def rotate(before, vectors):
        change = lax.dot_general(
            vectors, scaled_t[...], (((1,), (1,)), ((), ())), preferred_element_type=f32
        )
        return (before.astype(f32) - change).astype(bf16)

    span = capacity * TILE
    tile_copies = []
    here = pl.ds(pl.multiple_of(me * span, span), span)
    for d in list(range(1, peers)) + [0]:
        peer, where = in_plane(d)
        for j in range(capacity):
            tile = send_ref[me, j, peer]
            outbox[d, j * TILE : (j + 1) * TILE, :] = rotate(coeffs_v[tile], refl_v[tile])
        if d == 0:
            arrived[here, :] = outbox[0]
            continue
        copy = pltpu.make_async_remote_copy(
            src_ref=outbox.at[d],
            dst_ref=arrived.at[here],
            send_sem=tile_send.at[d],
            recv_sem=tile_recv.at[d],
            device_id=where,
            device_id_type=MESH,
        )
        copy.start()
        tile_copies.append(copy)

    def emit(i):
        at = pl.ds(pl.multiple_of(i * EMIT, EMIT), EMIT)
        return pltpu.make_async_copy(rot_v.at[at], rot_hbm.at[at], emit_sem.at[i])

    @pl.loop(0, emits)
    def _(i):
        at = pl.ds(pl.multiple_of(i * EMIT, EMIT), EMIT)
        some = pl.ds(i * (EMIT // TILE), EMIT // TILE)
        rot_v[at, :] = rotate(
            coeffs_v[some].reshape(EMIT, width), refl_v[some].reshape(EMIT, refl_v.shape[2])
        )
        emit(i).start()

    for d in range(2, n_col):
        fill_col(d)

    def add(q, first):
        deep = pl.ds(pl.multiple_of(q * span, span), span)

        @pl.loop(0, n_col)
        def _(j):
            at = pl.ds(pl.multiple_of(j * boxes * LANES, LANES), boxes * LANES)
            part = jnp.dot(phi[at, deep], arrived[deep, :], preferred_element_type=f32)
            orbitals[at, :] = part if first else orbitals[at, :] + part

    add(me, True)
    for d in range(1, peers):
        tile_copies[d - 1].wait()
        add(lax.rem(me + peers - d, peers), False)

    lanes = lax.broadcasted_iota(jnp.int32, (LANES, LANES), 1)
    dens_copies = []
    for d in list(range(1, n_col)) + [0]:
        peer, where = in_col(d)
        tall = boxes * LANES
        at = pl.ds(pl.multiple_of(peer * tall, tall), tall)
        orbital = orbitals[at, :]
        summed = jnp.sum(orbital * orbital, axis=1, keepdims=True)
        turned = jnp.zeros((LANES, LANES), f32)
        for b in range(boxes):
            turned = jnp.where(lanes == b, summed[b * LANES : (b + 1) * LANES], turned)
        dens_own[d] = turned.T[0:8, :]
        if d == 0:
            continue
        copy = pltpu.make_async_remote_copy(
            src_ref=dens_own.at[d],
            dst_ref=dens_got.at[d],
            send_sem=dens_send.at[d],
            recv_sem=dens_recv.at[d],
            device_id=where,
            device_id_type=MESH,
        )
        copy.start()
        dens_copies.append(copy)
    total = dens_own[0]
    for d in range(1, n_col):
        dens_copies[d - 1].wait()
        total = total + dens_got[d]
    dens_ref[...] = total[0:boxes, :] * (1.0 / (K * TILE))

    @pl.loop(0, emits)
    def _(i):
        emit(i).wait()


def fits(coeffs, reflectors, atom_pos, point_pos, send_tiles, sizes):
    n_row, n_box, n_col = sizes
    peers = n_row * n_box
    rows, width = coeffs.shape
    boxes = point_pos.shape[1]
    slots = peers * send_tiles.shape[2]
    return (
        width == LANES
        and rows % LOAD == 0
        and rows % EMIT == 0
        and rows * (reflectors.shape[1] + 2 * width) <= 16 << 20
        and reflectors.shape[1] % LANES == 0
        and width % peers == 0
        and (width // peers) % 16 == 0
        and boxes == 4
        and n_col <= 8
        and point_pos.shape[2] == LANES
        and atom_pos.shape[1] % LANES == 0
        and slots <= LANES
        and n_col * boxes * slots <= 512
        and n_col >= 2
    )


def per_device(
    coeffs,
    reflectors,
    factor,
    func_exp,
    func_atom,
    atom_pos,
    point_pos,
    send_tiles,
    box_tiles,
    box_count,
):
    sizes = lax.axis_size("row"), lax.axis_size("box"), lax.axis_size("col")
    if not fits(coeffs, reflectors, atom_pos, point_pos, send_tiles, sizes):
        return general(
            coeffs,
            reflectors,
            factor,
            func_exp,
            func_atom,
            atom_pos,
            point_pos,
            send_tiles,
            box_tiles,
            box_count,
        )
    n_row, n_box, n_col = sizes
    peers = n_row * n_box
    rows, width = coeffs.shape
    nref = reflectors.shape[1]
    boxes = point_pos.shape[1]
    capacity = send_tiles.shape[2]
    slots = peers * capacity
    f32, bf16 = jnp.float32, jnp.bfloat16
    vmem = pl.BlockSpec(memory_space=pltpu.VMEM)
    hbm = pl.BlockSpec(memory_space=pltpu.HBM)
    anywhere = pl.BlockSpec(memory_space=pl.ANY)
    dma = pltpu.SemaphoreType.DMA
    rotated, density = pl.pallas_call(
        functools.partial(kernel, n_row, n_box, n_col),
        out_shape=(
            jax.ShapeDtypeStruct((rows, width), bf16),
            jax.ShapeDtypeStruct((boxes, LANES), f32),
        ),
        in_specs=[hbm] * 10,
        out_specs=(anywhere, vmem),
        scratch_shapes=[
            pltpu.VMEM((rows // TILE, TILE, width), bf16),
            pltpu.VMEM((rows // TILE, TILE, nref), bf16),
            pltpu.VMEM((rows, width), bf16),
            pltpu.VMEM((width, nref), f32),
            pltpu.VMEM((width, nref), bf16),
            pltpu.VMEM((peers, width // peers, nref), bf16),
            pltpu.VMEM((width, nref), bf16),
            pltpu.VMEM((peers, capacity * TILE, width), bf16),
            pltpu.VMEM((slots * TILE, width), bf16),
            pltpu.VMEM((n_col * 16, LANES), f32),
            pltpu.VMEM((n_col * boxes, 4, LANES, LANES), f32),
            pltpu.VMEM((slots, 8, 2 * LANES), f32),
            pltpu.VMEM((slots, 8, LANES), f32),
            pltpu.VMEM((n_col * boxes * LANES, slots * TILE), bf16),
            pltpu.VMEM((n_col, 8, LANES), f32),
            pltpu.VMEM((n_col, 8, LANES), f32),
            pltpu.VMEM(point_pos.shape, f32),
            pltpu.SMEM((peers, capacity, peers), jnp.int32),
            pltpu.SMEM(box_tiles.shape, jnp.int32),
            pltpu.SMEM(box_count.shape, jnp.int32),
            pltpu.VMEM((n_col * boxes * LANES, width), f32),
            pltpu.VMEM(factor.shape, f32),
            pltpu.VMEM((func_exp.shape[0] // TILE, TILE), f32),
            pltpu.VMEM((func_exp.shape[0] // TILE, TILE), jnp.int32),
            pltpu.VMEM(atom_pos.shape, f32),
            pltpu.VMEM((atom_pos.shape[1] // LANES, 8, LANES), f32),
            dma((8,)),
            dma((2 * (rows // LOAD),)),
            dma((rows // EMIT,)),
            dma((n_col,)),
            dma((n_col,)),
            dma((peers,)),
            dma((peers,)),
            dma((peers,)),
            dma((peers,)),
            dma((peers,)),
            dma((peers,)),
            dma((n_col,)),
            dma((n_col,)),
        ],
        compiler_params=pltpu.CompilerParams(
            collective_id=0, has_side_effects=True, vmem_limit_bytes=63 << 20
        ),
        name="panel_and_density",
    )(
        coeffs.reshape(-1, TILE, width),
        reflectors.reshape(-1, TILE, nref),
        factor,
        func_exp.reshape(-1, TILE),
        func_atom.reshape(-1, TILE),
        atom_pos,
        point_pos,
        jnp.swapaxes(send_tiles, 1, 2),
        box_tiles,
        box_count,
    )
    return rotated, density


def solution(mesh):
    in_specs = (
        P(("row", "box"), "col"),
        P(("row", "box"), None),
        P(),
        P(),
        P(),
        P(),
        P(None, ("row", "col", "box"), None),
        P(),
        P(("row", "col", "box"), None),
        P(("row", "col", "box")),
    )
    out_specs = (P(("row", "box"), "col"), P(("row", "col", "box"), None))
    return jax.shard_map(
        per_device, mesh=mesh, in_specs=in_specs, out_specs=out_specs, check_vma=False
    )
```
